32 devices in a mesh: grp: 2 (over y), row: 4 (over x, core), slab: 4 (over z).
Axes of the slice: x: 2, y: 2, z: 4, core: 2. Of those that a mesh axis runs over, the one named last changes fastest.
Arguments:
- observed: float32 [128, 256, 256], P(('grp', 'slab'), 'row'), parts along dimension 0, may hold values from 0.25 to 4
- band_index: int32 [64], P('slab'), may hold values from 0 to 15
- taps_x: float32 [16, 31], replicated, may hold values from 0.005 to 0.12
- taps_y: float32 [16, 31], replicated, may hold values from 0.005 to 0.12
- taps_z: float32 [31], replicated, may hold values from 0.005 to 0.12
Outputs:
- estimate: float32 [128, 256, 256], P(('grp', 'slab'), 'row'), parts along dimension 0
The draws below stay inside these ranges and needn't reach their ends.
There are 2 independent parts, one for each index of `grp`. The reference program is written for one: setup_inputs(seed, part) draws one part's arguments, and reference() takes and returns one part's arrays. A program takes and returns all parts, laid end to end along the dimension named above; an argument that names none is the same for every part. Nothing has to cross between parts.
All inputs are finite; a program needn't handle non-finite values.
Results may differ from the reference program's by a relative error of at most 0.00015.
Values sent between devices are 32-bit elements; how exact they have to be, the bound alone decides.
A program may use at most 64 MiB of HBM per device.

```python
import math
import jax
import jax.numpy as jnp
from jax import lax

NY = 256
TAPS = 31
NB = 16
ITERS = 2
NX = 256
NZ = 64


def plant(array, key, least, top_value):
    extent = array.shape
    place = [jax.random.randint(jax.random.fold_in(key, axis), (), 0, extent[axis]) for axis in range(len(extent))]
    array = array.at[tuple(place)].set(least)
    longest = extent.index(max(extent))
    place[longest] = (place[longest] + 1) % extent[longest]
    return array.at[tuple(place)].set(top_value)


def block_scale(own_key, extent, pieces, low, top_value):
    gain = 1.0
    for position, parts in pieces:
        heights = jax.random.uniform(jax.random.fold_in(jax.random.fold_in(own_key, 6), position), (parts,), jnp.float32, low / len(pieces), top_value / len(pieces))
        gain = gain * jnp.repeat(jnp.exp(heights), extent[position] // parts).reshape((-1,) + (1,) * (len(extent) - 1 - position))
    return gain


def setup_inputs(seed: int = 0, part: int = 0) -> dict:
    keys = jax.random.split(jax.random.key(seed), 6)
    own_keys = jax.random.split(jax.random.fold_in(keys[5], part), 6)
    return {
        "observed": jnp.clip(0.25 + 3.75 * jax.random.uniform(own_keys[0], (NZ, NX, NY), jnp.float32) ** block_scale(own_keys[0], (NZ, NX, NY), ((0, 4), (1, 4)), -0.2, 0.2), 0.25, 4.0),
        "band_index": plant(jax.random.randint(keys[1], (NZ,), 0, NB), jax.random.fold_in(keys[1], 1), 0, NB - 1).astype(jnp.int32),
        "taps_x": jnp.clip(jnp.exp(jax.random.uniform(keys[2], (NB, TAPS), jnp.float32, math.log(0.005), math.log(0.12))), 0.005, 0.12),
        "taps_y": jnp.clip(jnp.exp(jax.random.uniform(keys[3], (NB, TAPS), jnp.float32, math.log(0.005), math.log(0.12))), 0.005, 0.12),
        "taps_z": jnp.clip(jnp.exp(jax.random.uniform(keys[4], (TAPS,), jnp.float32, math.log(0.005), math.log(0.12))), 0.005, 0.12),
    }


def correlate(field, taps, dim):
    radius = taps.shape[-1] // 2
    length = field.shape[dim]
    widths = [(0, 0), (0, 0), (0, 0)]
    widths[dim] = (radius, radius)
    padded = jnp.pad(field, widths)
    total = jnp.zeros(field.shape, jnp.float32)
    for k in range(taps.shape[-1]):
        piece = lax.slice_in_dim(padded, k, k + length, axis=dim)
        if taps.ndim == 2:
            weight = taps[:, k][:, None, None]
        else:
            weight = taps[k]
        total = total + weight * piece
    return total


def forward(field, plane_x, plane_y, taps_z):
    field = correlate(field, plane_x, 1)
    field = correlate(field, plane_y, 2)
    return correlate(field, taps_z, 0)


def adjoint(field, plane_x, plane_y, taps_z):
    field = correlate(field, taps_z[::-1], 0)
    field = correlate(field, plane_y[:, ::-1], 2)
    return correlate(field, plane_x[:, ::-1], 1)


def reference(observed, band_index, taps_x, taps_y, taps_z):
    plane_x = taps_x[band_index]
    plane_y = taps_y[band_index]
    norm = adjoint(jnp.ones(observed.shape, jnp.float32), plane_x, plane_y, taps_z)
    estimate = observed
    for step in range(ITERS):
        blurred = forward(estimate, plane_x, plane_y, taps_z)
        ratio = observed / blurred
        estimate = estimate * adjoint(ratio, plane_x, plane_y, taps_z) / norm
    return estimate
```

```python
import functools

import jax
import jax.numpy as jnp
from jax import lax
from jax.experimental import pallas as pl
from jax.experimental.pallas import tpu as pltpu
from jax.sharding import PartitionSpec as P

ITERS = 2
CHUNK = 16
F32 = jnp.float32
BF16 = jnp.bfloat16


def split(v):
    high = v.astype(BF16)
    return high, (v - high.astype(F32)).astype(BF16)


def chunk_order(count):
    if count < 4:
        return list(range(count))
    return [1, 0, count - 1] + list(range(2, count - 1))


def kernel(
    rows_n, slabs_n, taps,
    band_ref, tz_ref, tzv_ref, txf_ref, txr_ref, tyf_ref, tyr_ref, obs_ref,
    out_ref,
    ext, dext, bz, rz, wf_h, wf_l, wa_h, wa_l, af, aa,
    zs_sem, zr_sem, xs_sem, xr_sem,
):
    depth, height, width = obs_ref.shape
    radius = taps // 2
    halo = CHUNK
    chunks = height // CHUNK
    order = chunk_order(chunks)
    row = lax.axis_index("row")
    slab = lax.axis_index("slab")

    sides = {
        ("row", 0): (row < rows_n - 1, row + 1),
        ("row", 1): (row > 0, row - 1),
        ("slab", 0): (slab < slabs_n - 1, slab + 1),
        ("slab", 1): (slab > 0, slab - 1),
    }

    barrier = pltpu.get_barrier_semaphore()
    for (axis, _), (there, index) in sides.items():
        @pl.when(there)
        def _(axis=axis, index=index):
            pl.semaphore_signal(barrier, inc=1, device_id={axis: index}, device_id_type=pl.DeviceIdType.MESH)

    for (axis, side), buffers in (
        (("row", 1), (ext, dext)), (("row", 0), (ext, dext)),
        (("slab", 1), (bz, rz)), (("slab", 0), (bz, rz)),
    ):
        @pl.when(jnp.logical_not(sides[(axis, side)][0]))
        def _(axis=axis, side=side, buffers=buffers):
            for buffer in buffers:
                for it in range(ITERS):
                    if axis == "row":
                        start = 0 if side == 1 else halo + height
                        buffer[it, :, start:start + halo, :] = jnp.zeros((depth, halo, width), F32)
                    else:
                        start = 0 if side == 1 else radius + depth
                        buffer[it, start:start + radius] = jnp.zeros((radius, height, width), F32)

    pl.semaphore_wait(barrier, sum(there.astype(jnp.int32) for there, _ in sides.values()))

    def row_copy(src, dst, it, which, side):
        if side == 0:
            src_start, dst_start = src[1] + height - halo, 0
        else:
            src_start, dst_start = src[1], halo + height
        return pltpu.make_async_remote_copy(
            src_ref=src[0].at[:, pl.ds(src_start, halo), :],
            dst_ref=dst.at[it, :, pl.ds(dst_start, halo), :],
            send_sem=xs_sem.at[it, which, side],
            recv_sem=xr_sem.at[it, which, side],
            device_id={"row": sides[("row", side)][1]},
            device_id_type=pl.DeviceIdType.MESH,
        )

    def slab_copy(buf, it, which, c, side):
        if side == 0:
            src_start, dst_start = depth, 0
        else:
            src_start, dst_start = radius, radius + depth
        span = pl.ds(c * CHUNK, CHUNK)
        return pltpu.make_async_remote_copy(
            src_ref=buf.at[it, pl.ds(src_start, radius), span, :],
            dst_ref=buf.at[it, pl.ds(dst_start, radius), span, :],
            send_sem=zs_sem.at[it, which, c, side],
            recv_sem=zr_sem.at[it, which, c, side],
            device_id={"slab": sides[("slab", side)][1]},
            device_id_type=pl.DeviceIdType.MESH,
        )

    def start(axis, side, make):
        @pl.when(sides[(axis, side)][0])
        def _():
            make(side).start()

    def recv(axis, side, make):
        @pl.when(sides[(axis, 1 - side)][0])
        def _():
            make(side).wait_recv()

    def sent(axis, side, make):
        @pl.when(sides[(axis, side)][0])
        def _():
            make(side).wait_send()

    sends = []

    def x_make(it, which):
        if which == 0:
            src = (obs_ref, 0) if it == 0 else (ext.at[it], halo)
            return functools.partial(row_copy, src, ext, it, which)
        return functools.partial(row_copy, (dext.at[it], halo), dext, it, which)

    def z_make(it, which, c):
        return functools.partial(slab_copy, bz if which == 0 else rz, it, which, c)

    def x_start(it, which, side):
        start("row", side, x_make(it, which))
        sends.append(("row", side, x_make(it, which)))

    def z_start(it, which, c):
        for side in range(2):
            start("slab", side, z_make(it, which, c))
            sends.append(("slab", side, z_make(it, which, c)))

    def z_recv(it, which, c):
        for side in range(2):
            recv("slab", side, z_make(it, which, c))

    for side in range(2):
        x_start(0, 0, side)

    ext[0, :, halo:halo + height, :] = obs_ref[...]

    kk = 3 * halo

    def build_forward(z, carry):
        band = band_ref[z]
        line = jnp.broadcast_to(tyr_ref[band], (width, width))
        w = pltpu.roll(line, width - radius, 1, stride=1, stride_axis=0)
        near = lax.broadcasted_iota(jnp.int32, (width, width), 0) - lax.broadcasted_iota(jnp.int32, (width, width), 1)
        w = jnp.where((near <= radius) & (near >= -radius), w, 0.0)
        wf_h[z], wf_l[z] = split(w)
        a = jnp.broadcast_to(txf_ref[band], (CHUNK, width))
        a = pltpu.roll(a, halo - radius, 1, stride=1, stride_axis=0)
        high = a.astype(BF16).astype(F32)
        af[z] = (high + pltpu.roll(a - high, kk, 1) + pltpu.roll(high, 2 * kk, 1)).astype(BF16)
        return carry

    def build_adjoint(z, carry):
        band = band_ref[z]
        line = jnp.broadcast_to(tyf_ref[band], (width, width))
        w = pltpu.roll(line, width - radius, 1, stride=1, stride_axis=0)
        near = lax.broadcasted_iota(jnp.int32, (width, width), 0) - lax.broadcasted_iota(jnp.int32, (width, width), 1)
        w = jnp.where((near <= radius) & (near >= -radius), w, 0.0)
        plane = slab * depth + z + radius - lax.broadcasted_iota(jnp.int32, (1, 128), 1)
        inside = (plane >= 0) & (plane < slabs_n * depth)
        cz = jnp.sum(jnp.where(inside, tzv_ref[...], 0.0), axis=1, keepdims=True)
        w = w / (jnp.sum(w, axis=0, keepdims=True) * cz)
        wa_h[z], wa_l[z] = split(w)
        base = jnp.broadcast_to(txr_ref[band], (CHUNK, width))
        base = pltpu.roll(base, halo - radius, 1, stride=1, stride_axis=0)
        for c in range(chunks):
            at = row * height + (c - 1) * CHUNK + lax.broadcasted_iota(jnp.int32, (CHUNK, width), 1)
            inside = (at >= 0) & (at < rows_n * height)
            a = base / jnp.sum(jnp.where(inside, base, 0.0), axis=1, keepdims=True)
            high = a.astype(BF16).astype(F32)
            aa[z, c] = (high + pltpu.roll(a - high, kk, 1) + pltpu.roll(high, 2 * kk, 1)).astype(BF16)
        return carry

    def blur_rows(a, v):
        high, low = split(v)
        return jnp.dot(a[:, :3 * kk], jnp.concatenate([high, high, low], axis=0), preferred_element_type=F32)

    def blur_columns(v, w_h, w_l):
        high, low = split(v)
        n = v.shape[0]
        both = jnp.dot(jnp.concatenate([high, low], axis=0), w_h, preferred_element_type=F32)
        return both[:n] + both[n:] + jnp.dot(high, w_l, preferred_element_type=F32)

    def stage_xy(it, c):
        def body(z, carry):
            v = blur_rows(af[z], ext[it, z, c * CHUNK:c * CHUNK + kk, :])
            bz[it, radius + z, c * CHUNK:(c + 1) * CHUNK, :] = blur_columns(v, wf_h[z], wf_l[z])
            return carry
        lax.fori_loop(0, depth, body, 0, unroll=4)

    def blur_depth(buf, it, tile, lanes, flip):
        total = None
        for k in range(taps):
            weight = tz_ref[taps - 1 - k] if flip else tz_ref[k]
            term = weight * buf[it, k:k + depth, tile, lanes]
            total = term if total is None else total + term
        return total

    def tiles(c):
        for r in range(CHUNK // 8):
            for l in range(width // 128):
                yield slice(c * CHUNK + r * 8, c * CHUNK + r * 8 + 8), slice(l * 128, l * 128 + 128)

    def stage_ratio(it, c):
        for tile, lanes in tiles(c):
            rz[it, radius:radius + depth, tile, lanes] = obs_ref[:, tile, lanes] / blur_depth(bz, it, tile, lanes, False)

    def stage_zy(it, c):
        inner = slice(halo + c * CHUNK, halo + (c + 1) * CHUNK)
        for tile, lanes in tiles(c):
            target = slice(halo + tile.start, halo + tile.stop)
            dext[it, :, target, lanes] = blur_depth(rz, it, tile, lanes, True)

        def body(z, carry):
            dext[it, z, inner, :] = blur_columns(dext[it, z, inner, :], wa_h[z], wa_l[z])
            return carry
        lax.fori_loop(0, depth, body, 0, unroll=4)

    def stage_x(it, c):
        span = slice(c * CHUNK, (c + 1) * CHUNK)
        inner = slice(halo + c * CHUNK, halo + (c + 1) * CHUNK)

        def body(z, carry):
            v = ext[it, z, inner, :] * blur_rows(aa[z, c], dext[it, z, c * CHUNK:c * CHUNK + kk, :])
            if it == ITERS - 1:
                out_ref[z, span, :] = v
            else:
                ext[it + 1, z, inner, :] = v
            return carry
        lax.fori_loop(0, depth, body, 0, unroll=4)

    lax.fori_loop(0, depth, build_forward, 0)
    for it in range(ITERS):
        for c in order:
            if c == 0:
                recv("row", 0, x_make(it, 0))
            if c == chunks - 1:
                recv("row", 1, x_make(it, 0))
            stage_xy(it, c)
            z_start(it, 0, c)
        if it == 0:
            lax.fori_loop(0, depth, build_adjoint, 0)
        for c in order:
            z_recv(it, 0, c)
            stage_ratio(it, c)
            z_start(it, 1, c)
        for c in order:
            z_recv(it, 1, c)
            stage_zy(it, c)
            if c == 0:
                x_start(it, 1, 1)
            if c == chunks - 1:
                x_start(it, 1, 0)
        for c in [0, chunks - 1] + list(range(1, chunks - 1)):
            if c == 0:
                recv("row", 0, x_make(it, 1))
            if c == chunks - 1:
                recv("row", 1, x_make(it, 1))
            stage_x(it, c)
            if it < ITERS - 1:
                if c == 0:
                    x_start(it + 1, 0, 1)
                if c == chunks - 1:
                    x_start(it + 1, 0, 0)

    for axis, side, make in sends:
        sent(axis, side, make)


def solution(mesh):
    rows_n, slabs_n = mesh.shape["row"], mesh.shape["slab"]

    def on_device(observed, band_index, taps_x, taps_y, taps_z):
        depth, height, width = observed.shape
        bands, taps = taps_x.shape
        radius = taps // 2

        def padded(t):
            return jnp.pad(t, ((0, 0), (0, width - taps)))[:, None, :]

        tzv = jnp.pad(taps_z, (0, 128 - taps))[None, :]
        vmem = pl.BlockSpec(memory_space=pltpu.VMEM)
        smem = pl.BlockSpec(memory_space=pltpu.SMEM)
        chunks = height // CHUNK
        return pl.pallas_call(
            functools.partial(kernel, rows_n, slabs_n, taps),
            out_shape=jax.ShapeDtypeStruct(observed.shape, F32),
            in_specs=[smem, smem] + [vmem] * 6,
            out_specs=vmem,
            scratch_shapes=[
                pltpu.VMEM((ITERS, depth, height + 2 * CHUNK, width), F32),
                pltpu.VMEM((ITERS, depth, height + 2 * CHUNK, width), F32),
                pltpu.VMEM((ITERS, depth + 2 * radius, height, width), F32),
                pltpu.VMEM((ITERS, depth + 2 * radius, height, width), F32),
                pltpu.VMEM((depth, width, width), BF16),
                pltpu.VMEM((depth, width, width), BF16),
                pltpu.VMEM((depth, width, width), BF16),
                pltpu.VMEM((depth, width, width), BF16),
                pltpu.VMEM((depth, CHUNK, width), BF16),
                pltpu.VMEM((depth, chunks, CHUNK, width), BF16),
                pltpu.SemaphoreType.DMA((ITERS, 2, chunks, 2)),
                pltpu.SemaphoreType.DMA((ITERS, 2, chunks, 2)),
                pltpu.SemaphoreType.DMA((ITERS, 2, 2)),
                pltpu.SemaphoreType.DMA((ITERS, 2, 2)),
            ],
            compiler_params=pltpu.CompilerParams(
                collective_id=0, has_side_effects=True, vmem_limit_bytes=60 * 1024 * 1024
            ),
        )(
            band_index, taps_z, tzv,
            padded(taps_x), padded(taps_x[:, ::-1]), padded(taps_y), padded(taps_y[:, ::-1]),
            observed,
        )

    in_specs = (P(("grp", "slab"), "row", None), P("slab"), P(), P(), P())
    return jax.shard_map(
        on_device, mesh=mesh, in_specs=in_specs, out_specs=P(("grp", "slab"), "row", None), check_vma=False
    )
```

```python
import functools

import jax
import jax.numpy as jnp
from jax import lax
from jax.experimental import pallas as pl
from jax.experimental.pallas import tpu as pltpu
from jax.sharding import PartitionSpec as P

ITERS = 2
CHUNK = 16
LANES = 128
F32 = jnp.float32
BF16 = jnp.bfloat16


def split(v):
    high = v.astype(BF16)
    return high, (v - high.astype(F32)).astype(BF16)


def chunk_order(count):
    if count < 4:
        return list(range(count))
    return [1, 0, count - 1] + list(range(2, count - 1))


def kernel(
    rows_n, slabs_n, taps,
    band_ref, tz_ref, tx_ref, ty_ref, obs_ref,
    out_ref,
    txf_ref, txr_ref, tyf_ref, tyr_ref, ext, dext, bz, rz, wf_h, wf_l, wa_h, wa_l, af, aa,
    zs_sem, zr_sem, xs_sem, xr_sem,
):
    depth, height, width = obs_ref.shape
    radius = taps // 2
    halo = CHUNK
    chunks = height // CHUNK
    order = chunk_order(chunks)
    row = lax.axis_index("row")
    slab = lax.axis_index("slab")

    sides = {
        ("row", 0): (row < rows_n - 1, row + 1),
        ("row", 1): (row > 0, row - 1),
        ("slab", 0): (slab < slabs_n - 1, slab + 1),
        ("slab", 1): (slab > 0, slab - 1),
    }

    barrier = pltpu.get_barrier_semaphore()
    for (axis, _), (there, index) in sides.items():
        @pl.when(there)
        def _(axis=axis, index=index):
            pl.semaphore_signal(barrier, inc=1, device_id={axis: index}, device_id_type=pl.DeviceIdType.MESH)

    def clear(axis, buffer, it):
        for side in range(2):
            @pl.when(jnp.logical_not(sides[(axis, side)][0]))
            def _():
                if axis == "row":
                    first = 0 if side == 1 else halo + height
                    buffer[it, :, first:first + halo, :] = jnp.zeros((depth, halo, width), F32)
                else:
                    first = 0 if side == 1 else radius + depth
                    buffer[it, first:first + radius] = jnp.zeros((radius, height, width), F32)

    pl.semaphore_wait(barrier, sum(there.astype(jnp.int32) for there, _ in sides.values()))

    def row_copy(src, dst, it, which, side):
        if side == 0:
            src_start, dst_start = src[1] + height - halo, 0
        else:
            src_start, dst_start = src[1], halo + height
        return pltpu.make_async_remote_copy(
            src_ref=src[0].at[:, pl.ds(src_start, halo), :],
            dst_ref=dst.at[it, :, pl.ds(dst_start, halo), :],
            send_sem=xs_sem.at[it, which, side],
            recv_sem=xr_sem.at[it, which, side],
            device_id={"row": sides[("row", side)][1]},
            device_id_type=pl.DeviceIdType.MESH,
        )

    def slab_copy(buf, it, which, c, side):
        if side == 0:
            src_start, dst_start = depth, 0
        else:
            src_start, dst_start = radius, radius + depth
        span = pl.ds(c * CHUNK, CHUNK)
        return pltpu.make_async_remote_copy(
            src_ref=buf.at[it, pl.ds(src_start, radius), span, :],
            dst_ref=buf.at[it, pl.ds(dst_start, radius), span, :],
            send_sem=zs_sem.at[it, which, c, side],
            recv_sem=zr_sem.at[it, which, c, side],
            device_id={"slab": sides[("slab", side)][1]},
            device_id_type=pl.DeviceIdType.MESH,
        )

    def start(axis, side, make):
        @pl.when(sides[(axis, side)][0])
        def _():
            make(side).start()

    def recv(axis, side, make):
        @pl.when(sides[(axis, 1 - side)][0])
        def _():
            make(side).wait_recv()

    def sent(axis, side, make):
        @pl.when(sides[(axis, side)][0])
        def _():
            make(side).wait_send()

    sends = []

    def x_make(it, which):
        if which == 0:
            src = (obs_ref, 0) if it == 0 else (ext.at[it], halo)
            return functools.partial(row_copy, src, ext, it, which)
        return functools.partial(row_copy, (dext.at[it], halo), dext, it, which)

    def z_make(it, which, c):
        return functools.partial(slab_copy, bz if which == 0 else rz, it, which, c)

    def x_start(it, which, side):
        start("row", side, x_make(it, which))
        sends.append(("row", side, x_make(it, which)))

    def z_start(it, which, c):
        for side in range(2):
            start("slab", side, z_make(it, which, c))
            sends.append(("slab", side, z_make(it, which, c)))

    def z_recv(it, which, c):
        for side in range(2):
            recv("slab", side, z_make(it, which, c))

    for side in range(2):
        x_start(0, 0, side)

    ext[0, :, halo:halo + height, :] = obs_ref[...]

    kk = 3 * halo
    mirror = (
        lax.broadcasted_iota(jnp.int32, (LANES, LANES), 0) + lax.broadcasted_iota(jnp.int32, (LANES, LANES), 1)
        == taps - 1
    ).astype(F32)
    for source, ahead, back in ((tx_ref, txf_ref, txr_ref), (ty_ref, tyf_ref, tyr_ref)):
        ahead[...] = jnp.zeros(ahead.shape, F32)
        ahead[:, 0:taps] = source[...]
        back[...] = jnp.dot(ahead[...], mirror, precision=lax.Precision.HIGHEST, preferred_element_type=F32)

    gap = lax.broadcasted_iota(jnp.int32, (LANES, LANES), 0) - lax.broadcasted_iota(jnp.int32, (LANES, LANES), 1)
    blocks = range(width // LANES)

    def column_band(line):
        ring = pltpu.roll(jnp.broadcast_to(line, (LANES, LANES)), LANES - radius, 1, stride=1, stride_axis=0)

        def block(offset):
            near = gap + offset * LANES
            return jnp.where((near <= radius) & (near >= -radius), ring, 0.0)
        made = {offset: block(offset) for offset in (-1, 0, 1)}
        return [[made.get(i - j) for j in blocks] for i in blocks]

    def store_band(w_h, w_l, z, band, scale):
        for i in blocks:
            for j in blocks:
                part = jnp.zeros((LANES, LANES), F32) if band[i][j] is None else band[i][j]
                if scale is not None:
                    part = part * scale[j]
                high, low = split(part)
                w_h[z, i * LANES:(i + 1) * LANES, j * LANES:(j + 1) * LANES] = high
                w_l[z, i * LANES:(i + 1) * LANES, j * LANES:(j + 1) * LANES] = low

    def store_rows(a):
        high = a.astype(BF16).astype(F32)
        low = a - high
        zero = jnp.zeros(a.shape, F32)
        first = jnp.concatenate([high, zero], axis=1)
        second = jnp.concatenate([low, zero], axis=1)
        return (first + pltpu.roll(second, kk, 1) + pltpu.roll(first, 2 * kk, 1)).astype(BF16)

    def row_band(line):
        return pltpu.roll(jnp.broadcast_to(line, (CHUNK, LANES)), halo - radius, 1, stride=1, stride_axis=0)

    def build_forward(z, carry):
        at = pl.ds(band_ref[z], 1)
        store_band(wf_h, wf_l, z, column_band(tyr_ref[at, :]), None)
        af[z] = store_rows(row_band(txf_ref[at, :]))
        return carry

    def build_adjoint(z, carry):
        at = pl.ds(band_ref[z], 1)
        band = column_band(tyf_ref[at, :])
        lane = lax.broadcasted_iota(jnp.int32, (1, LANES), 1)
        tzv = jnp.zeros((1, LANES), F32)
        for k in range(taps):
            tzv = jnp.where(lane == k, tz_ref[k], tzv)
        plane = slab * depth + z + radius - lane
        inside = (plane >= 0) & (plane < slabs_n * depth)
        cz = jnp.sum(jnp.where(inside, tzv, 0.0), axis=1, keepdims=True)
        scale = []
        for j in blocks:
            total = sum(jnp.sum(band[i][j], axis=0, keepdims=True) for i in blocks if band[i][j] is not None)
            scale.append(1.0 / (total * cz))
        store_band(wa_h, wa_l, z, band, scale)
        base = row_band(txr_ref[at, :])
        for c in range(chunks):
            at_row = row * height + (c - 1) * CHUNK + lax.broadcasted_iota(jnp.int32, (CHUNK, LANES), 1)
            inside = (at_row >= 0) & (at_row < rows_n * height)
            aa[z, c] = store_rows(base / jnp.sum(jnp.where(inside, base, 0.0), axis=1, keepdims=True))
        return carry

    def blur_rows(a, v):
        high, low = split(v)
        return jnp.dot(a[:, :3 * kk], jnp.concatenate([high, high, low], axis=0), preferred_element_type=F32)

    def blur_columns(v, w_h, w_l):
        high, low = split(v)
        n = v.shape[0]
        both = jnp.dot(jnp.concatenate([high, low], axis=0), w_h, preferred_element_type=F32)
        return both[:n] + both[n:] + jnp.dot(high, w_l, preferred_element_type=F32)

    def stage_xy(it, c):
        def body(z, carry):
            v = blur_rows(af[z], ext[it, z, c * CHUNK:c * CHUNK + kk, :])
            bz[it, radius + z, c * CHUNK:(c + 1) * CHUNK, :] = blur_columns(v, wf_h[z], wf_l[z])
            return carry
        lax.fori_loop(0, depth, body, 0, unroll=4)

    def blur_depth(buf, it, tile, lanes, flip):
        total = None
        for k in range(taps):
            weight = tz_ref[taps - 1 - k] if flip else tz_ref[k]
            term = weight * buf[it, k:k + depth, tile, lanes]
            total = term if total is None else total + term
        return total

    def tiles(c):
        for r in range(CHUNK // 8):
            for l in range(width // 128):
                yield slice(c * CHUNK + r * 8, c * CHUNK + r * 8 + 8), slice(l * 128, l * 128 + 128)

    def stage_ratio(it, c):
        for tile, lanes in tiles(c):
            rz[it, radius:radius + depth, tile, lanes] = obs_ref[:, tile, lanes] / blur_depth(bz, it, tile, lanes, False)

    def stage_zy(it, c):
        inner = slice(halo + c * CHUNK, halo + (c + 1) * CHUNK)
        for tile, lanes in tiles(c):
            target = slice(halo + tile.start, halo + tile.stop)
            dext[it, :, target, lanes] = blur_depth(rz, it, tile, lanes, True)

        def body(z, carry):
            dext[it, z, inner, :] = blur_columns(dext[it, z, inner, :], wa_h[z], wa_l[z])
            return carry
        lax.fori_loop(0, depth, body, 0, unroll=4)

    def stage_x(it, c):
        span = slice(c * CHUNK, (c + 1) * CHUNK)
        inner = slice(halo + c * CHUNK, halo + (c + 1) * CHUNK)

        def body(z, carry):
            v = ext[it, z, inner, :] * blur_rows(aa[z, c], dext[it, z, c * CHUNK:c * CHUNK + kk, :])
            if it == ITERS - 1:
                out_ref[z, span, :] = v
            else:
                ext[it + 1, z, inner, :] = v
            return carry
        lax.fori_loop(0, depth, body, 0, unroll=4)

    clear("row", ext, 0)
    lax.fori_loop(0, depth, build_forward, 0, unroll=2)
    for it in range(ITERS):
        def edge_x(which, c, it=it):
            if c == 0:
                recv("row", 0, x_make(it, which))
            if c == chunks - 1:
                recv("row", 1, x_make(it, which))

        def back_x(c, it=it, edge_x=edge_x):
            edge_x(1, c)
            stage_x(it, c)
            if it < ITERS - 1:
                if c == 0:
                    x_start(it + 1, 0, 1)
                if c == chunks - 1:
                    x_start(it + 1, 0, 0)

        for n, c in enumerate(order):
            edge_x(0, c)
            stage_xy(it, c)
            z_start(it, 0, c)
            if n == 0 and it > 0:
                for extra in late:
                    late_x(extra)
        if it == 0:
            lax.fori_loop(0, depth, build_adjoint, 0)
            for buffer in (bz, rz):
                for i in range(ITERS):
                    clear("slab", buffer, i)
            for i in range(ITERS):
                clear("row", dext, i)
            for i in range(1, ITERS):
                clear("row", ext, i)
        for c in order:
            z_recv(it, 0, c)
            stage_ratio(it, c)
            z_start(it, 1, c)
        done, left = [], list(range(chunks))
        for n, c in enumerate(order):
            if n == chunks - 1:
                for e in list(left):
                    if all(near in done for near in (e - 1, e, e + 1) if 0 <= near < chunks):
                        back_x(e)
                        left.remove(e)
            z_recv(it, 1, c)
            stage_zy(it, c)
            done.append(c)
            if c == 0:
                x_start(it, 1, 1)
            if c == chunks - 1:
                x_start(it, 1, 0)
        needed = [e for e in left if abs(e - order[0]) <= 1]
        late = [e for e in left if e not in needed]
        late_x = back_x
        for e in needed:
            back_x(e)
        if it == ITERS - 1 or order[0] in (0, chunks - 1):
            for e in late:
                back_x(e)
            late = []

    for axis, side, make in sends:
        sent(axis, side, make)


def solution(mesh):
    rows_n, slabs_n = mesh.shape["row"], mesh.shape["slab"]

    def on_device(observed, band_index, taps_x, taps_y, taps_z):
        depth, height, width = observed.shape
        bands, taps = taps_x.shape
        radius = taps // 2

        vmem = pl.BlockSpec(memory_space=pltpu.VMEM)
        smem = pl.BlockSpec(memory_space=pltpu.SMEM)
        chunks = height // CHUNK
        return pl.pallas_call(
            functools.partial(kernel, rows_n, slabs_n, taps),
            out_shape=jax.ShapeDtypeStruct(observed.shape, F32),
            in_specs=[smem, smem] + [vmem] * 3,
            out_specs=vmem,
            scratch_shapes=[pltpu.VMEM((bands, LANES), F32)] * 4 + [
                pltpu.VMEM((ITERS, depth, height + 2 * CHUNK, width), F32),
                pltpu.VMEM((ITERS, depth, height + 2 * CHUNK, width), F32),
                pltpu.VMEM((ITERS, depth + 2 * radius, height, width), F32),
                pltpu.VMEM((ITERS, depth + 2 * radius, height, width), F32),
                pltpu.VMEM((depth, width, width), BF16),
                pltpu.VMEM((depth, width, width), BF16),
                pltpu.VMEM((depth, width, width), BF16),
                pltpu.VMEM((depth, width, width), BF16),
                pltpu.VMEM((depth, CHUNK, width), BF16),
                pltpu.VMEM((depth, chunks, CHUNK, width), BF16),
                pltpu.SemaphoreType.DMA((ITERS, 2, chunks, 2)),
                pltpu.SemaphoreType.DMA((ITERS, 2, chunks, 2)),
                pltpu.SemaphoreType.DMA((ITERS, 2, 2)),
                pltpu.SemaphoreType.DMA((ITERS, 2, 2)),
            ],
            compiler_params=pltpu.CompilerParams(
                collective_id=0, has_side_effects=True, vmem_limit_bytes=40 * 1024 * 1024
            ),
        )(
            band_index, taps_z, taps_x, taps_y,
            observed,
        )

    in_specs = (P(("grp", "slab"), "row", None), P("slab"), P(), P(), P())
    return jax.shard_map(
        on_device, mesh=mesh, in_specs=in_specs, out_specs=P(("grp", "slab"), "row", None), check_vma=False
    )
```

```python
import functools

import jax
import jax.numpy as jnp
from jax import lax
from jax.experimental import pallas as pl
from jax.experimental.pallas import tpu as pltpu
from jax.sharding import PartitionSpec as P

ITERS = 2
CHUNK = 16
LANES = 128
F32 = jnp.float32
BF16 = jnp.bfloat16


def split(v):
    high = v.astype(BF16)
    return high, (v - high.astype(F32)).astype(BF16)


def chunk_order(count, it):
    first = [1, 0] if it == 0 else [0, 1]
    inner = list(range(2, count - 1))
    return first + ([count - 1] + inner if it == ITERS - 1 else inner + [count - 1])


def kernel(
    rows_n, slabs_n, taps,
    band_hbm, tz_hbm, tx_hbm, ty_hbm, obs_hbm,
    out_ref,
    band_ref, tz_ref, tx_ref, ty_ref, in_sem,
    txf_ref, txr_ref, tyf_ref, tyr_ref, ext, dext, bz, rz, wf_h, wf_l, wa_h, wa_l, af, aa,
    zs_sem, zr_sem, xs_sem, xr_sem,
):
    depth, height, width = obs_hbm.shape
    radius = taps // 2
    halo = CHUNK
    chunks = height // CHUNK
    row = lax.axis_index("row")
    slab = lax.axis_index("slab")
    parity = row % 2

    def chunk(p):
        return p + parity * (chunks - 1 - 2 * p)

    def begin(p, more=0, unit=CHUNK):
        return pl.multiple_of(chunk(p) * CHUNK + more, unit)

    fetches = [
        pltpu.make_async_copy(src, dst, in_sem.at[n])
        for n, (src, dst) in enumerate((
            (obs_hbm, ext.at[0, :, pl.ds(halo, height), :]),
            (ty_hbm, ty_ref), (tx_hbm, tx_ref), (band_hbm, band_ref), (tz_hbm, tz_ref),
        ))
    ]
    for fetch in fetches:
        fetch.start()

    sides = {
        ("row", 0): (row < rows_n - 1, row + 1),
        ("row", 1): (row > 0, row - 1),
        ("slab", 0): (slab < slabs_n - 1, slab + 1),
        ("slab", 1): (slab > 0, slab - 1),
    }

    barrier = pltpu.get_barrier_semaphore()
    for (axis, _), (there, index) in sides.items():
        @pl.when(there)
        def _(axis=axis, index=index):
            pl.semaphore_signal(barrier, inc=1, device_id={axis: index}, device_id_type=pl.DeviceIdType.MESH)

    def clear(axis, buffer, it):
        for side in range(2):
            @pl.when(jnp.logical_not(sides[(axis, side)][0]))
            def _():
                if axis == "row":
                    first = 0 if side == 1 else halo + height
                    buffer[it, :, first:first + halo, :] = jnp.zeros((depth, halo, width), F32)
                else:
                    first = 0 if side == 1 else radius + depth
                    buffer[it, first:first + radius] = jnp.zeros((radius, height, width), F32)

    pl.semaphore_wait(barrier, sum(there.astype(jnp.int32) for there, _ in sides.values()))

    def row_copy(src, dst, it, which, side):
        if side == 0:
            src_start, dst_start = src[1] + height - halo, 0
        else:
            src_start, dst_start = src[1], halo + height
        return pltpu.make_async_remote_copy(
            src_ref=src[0].at[:, pl.ds(src_start, halo), :],
            dst_ref=dst.at[it, :, pl.ds(dst_start, halo), :],
            send_sem=xs_sem.at[it, which, side],
            recv_sem=xr_sem.at[it, which, side],
            device_id={"row": sides[("row", side)][1]},
            device_id_type=pl.DeviceIdType.MESH,
        )

    def slab_copy(buf, it, which, c, side):
        if side == 0:
            src_start, dst_start = depth, 0
        else:
            src_start, dst_start = radius, radius + depth
        span = pl.ds(begin(c), CHUNK)
        return pltpu.make_async_remote_copy(
            src_ref=buf.at[it, pl.ds(src_start, radius), span, :],
            dst_ref=buf.at[it, pl.ds(dst_start, radius), span, :],
            send_sem=zs_sem.at[it, which, c, side],
            recv_sem=zr_sem.at[it, which, c, side],
            device_id={"slab": sides[("slab", side)][1]},
            device_id_type=pl.DeviceIdType.MESH,
        )

    def start(axis, side, make, also=True):
        @pl.when(sides[(axis, side)][0] & also)
        def _():
            make(side).start()

    def recv(axis, side, make, also=True):
        @pl.when(sides[(axis, 1 - side)][0] & also)
        def _():
            make(side).wait_recv()

    def sent(axis, side, make):
        @pl.when(sides[(axis, side)][0])
        def _():
            make(side).wait_send()

    sends = []

    def x_make(it, which):
        buffer = ext if which == 0 else dext
        return functools.partial(row_copy, (buffer.at[it], halo), buffer, it, which)

    def z_make(it, which, c):
        return functools.partial(slab_copy, bz if which == 0 else rz, it, which, c)

    def x_start(it, which, p):
        near = p == 0
        for v in range(2):
            side = 1 - v if near else v
            start("row", side, x_make(it, which), parity == v)
        if near:
            sends.extend(("row", side, x_make(it, which)) for side in range(2))

    def x_recv(it, which, p):
        near = p == 0
        for v in range(2):
            recv("row", v if near else 1 - v, x_make(it, which), parity == v)

    def z_start(it, which, c):
        for side in range(2):
            start("slab", side, z_make(it, which, c))
            sends.append(("slab", side, z_make(it, which, c)))

    def z_recv(it, which, c):
        for side in range(2):
            recv("slab", side, z_make(it, which, c))

    fetches[0].wait()
    for p in (0, chunks - 1):
        x_start(0, 0, p)
    for fetch in fetches[1:]:
        fetch.wait()

    kk = 3 * halo
    mirror = (
        lax.broadcasted_iota(jnp.int32, (LANES, LANES), 0) + lax.broadcasted_iota(jnp.int32, (LANES, LANES), 1)
        == taps - 1
    ).astype(F32)
    for source, ahead, back in ((tx_ref, txf_ref, txr_ref), (ty_ref, tyf_ref, tyr_ref)):
        ahead[...] = jnp.zeros(ahead.shape, F32)
        ahead[:, 0:taps] = source[...]
        back[...] = jnp.dot(ahead[...], mirror, precision=lax.Precision.HIGHEST, preferred_element_type=F32)

    gap = lax.broadcasted_iota(jnp.int32, (LANES, LANES), 0) - lax.broadcasted_iota(jnp.int32, (LANES, LANES), 1)
    blocks = range(width // LANES)

    def column_band(line):
        ring = pltpu.roll(jnp.broadcast_to(line, (LANES, LANES)), LANES - radius, 1, stride=1, stride_axis=0)

        def block(offset):
            near = gap + offset * LANES
            return jnp.where((near <= radius) & (near >= -radius), ring, 0.0)
        made = {offset: block(offset) for offset in (-1, 0, 1)}
        return [[made.get(i - j) for j in blocks] for i in blocks]

    def store_band(w_h, w_l, z, band, scale):
        for i in blocks:
            for j in blocks:
                part = jnp.zeros((LANES, LANES), F32) if band[i][j] is None else band[i][j]
                if scale is not None:
                    part = part * scale[j]
                high, low = split(part)
                w_h[z, i * LANES:(i + 1) * LANES, j * LANES:(j + 1) * LANES] = high
                w_l[z, i * LANES:(i + 1) * LANES, j * LANES:(j + 1) * LANES] = low

    def store_rows(a):
        high = a.astype(BF16).astype(F32)
        low = a - high
        zero = jnp.zeros(a.shape, F32)
        first = jnp.concatenate([high, zero], axis=1)
        second = jnp.concatenate([low, zero], axis=1)
        return (first + pltpu.roll(second, kk, 1) + pltpu.roll(first, 2 * kk, 1)).astype(BF16)

    def row_band(line):
        return pltpu.roll(jnp.broadcast_to(line, (CHUNK, LANES)), halo - radius, 1, stride=1, stride_axis=0)

    def build_forward(z, carry):
        at = pl.ds(band_ref[z], 1)
        store_band(wf_h, wf_l, z, column_band(tyr_ref[at, :]), None)
        af[z] = store_rows(row_band(txf_ref[at, :]))
        return carry

    def build_adjoint(z, carry):
        at = pl.ds(band_ref[z], 1)
        band = column_band(tyf_ref[at, :])
        lane = lax.broadcasted_iota(jnp.int32, (1, LANES), 1)
        tzv = jnp.zeros((1, LANES), F32)
        for k in range(taps):
            tzv = jnp.where(lane == k, tz_ref[k], tzv)
        plane = slab * depth + z + radius - lane
        inside = (plane >= 0) & (plane < slabs_n * depth)
        cz = jnp.sum(jnp.where(inside, tzv, 0.0), axis=1, keepdims=True)
        scale = []
        for j in blocks:
            total = sum(jnp.sum(band[i][j], axis=0, keepdims=True) for i in blocks if band[i][j] is not None)
            scale.append(1.0 / (total * cz))
        store_band(wa_h, wa_l, z, band, scale)
        base = row_band(txr_ref[at, :])
        for c in range(chunks):
            at_row = row * height + (c - 1) * CHUNK + lax.broadcasted_iota(jnp.int32, (CHUNK, LANES), 1)
            inside = (at_row >= 0) & (at_row < rows_n * height)
            aa[z, c] = store_rows(base / jnp.sum(jnp.where(inside, base, 0.0), axis=1, keepdims=True))
        return carry

    def blur_rows(a, v):
        high, low = split(v)
        return jnp.dot(a[:, :3 * kk], jnp.concatenate([high, high, low], axis=0), preferred_element_type=F32)

    def blur_columns(v, w_h, w_l):
        high, low = split(v)
        n = v.shape[0]
        both = jnp.dot(jnp.concatenate([high, low], axis=0), w_h, preferred_element_type=F32)
        return both[:n] + both[n:] + jnp.dot(high, w_l, preferred_element_type=F32)

    def edge(it, which, p):
        if p in (0, chunks - 1):
            x_recv(it, which, p)

    def stage_xy(it, p):
        edge(it, 0, p)
        c = begin(p)

        def body(z, carry):
            v = blur_rows(af[z], ext[it, z, pl.ds(c, kk), :])
            bz[it, radius + z, pl.ds(c, CHUNK), :] = blur_columns(v, wf_h[z], wf_l[z])
            return carry
        lax.fori_loop(0, depth, body, 0, unroll=4)
        z_start(it, 0, p)

    def blur_depth(buf, it, tile, lanes, flip):
        total = None
        for k in range(taps):
            weight = tz_ref[taps - 1 - k] if flip else tz_ref[k]
            term = weight * buf[it, k:k + depth, tile, lanes]
            total = term if total is None else total + term
        return total

    def tiles(p):
        for r in range(0, CHUNK, 8):
            for l in range(0, width, LANES):
                yield pl.ds(begin(p, r, 8), 8), pl.ds(begin(p, halo + r, 8), 8), slice(l, l + LANES)

    def stage_ratio(it, p):
        for tile, inner, lanes in tiles(p):
            blurred = blur_depth(bz, it, tile, lanes, False)
            rz[it, radius:radius + depth, tile, lanes] = ext[0, :, inner, lanes] / blurred
        z_start(it, 1, p)

    def stage_zy(it, p):
        for tile, inner, lanes in tiles(p):
            dext[it, :, inner, lanes] = blur_depth(rz, it, tile, lanes, True)
        rows = pl.ds(begin(p, halo), CHUNK)

        def body(z, carry):
            dext[it, z, rows, :] = blur_columns(dext[it, z, rows, :], wa_h[z], wa_l[z])
            return carry
        lax.fori_loop(0, depth, body, 0, unroll=4)
        if p in (0, chunks - 1):
            x_start(it, 1, p)

    def stage_x(it, p):
        edge(it, 1, p)
        c = begin(p)
        inner = pl.ds(begin(p, halo), CHUNK)

        def body(z, carry):
            v = ext[it, z, inner, :] * blur_rows(aa[z, chunk(p)], dext[it, z, pl.ds(c, kk), :])
            if it == ITERS - 1:
                out_ref[z, pl.ds(c, CHUNK), :] = v
            else:
                ext[it + 1, z, inner, :] = v
            return carry
        lax.fori_loop(0, depth, body, 0, unroll=4)
        if it < ITERS - 1 and p in (0, chunks - 1):
            x_start(it + 1, 0, p)

    clear("row", ext, 0)
    lax.fori_loop(0, depth, build_forward, 0, unroll=2)
    started = 0
    for it in range(ITERS):
        order = chunk_order(chunks, it)
        for p in order[started:]:
            stage_xy(it, p)
        if it == 0:
            lax.fori_loop(0, depth, build_adjoint, 0)
            for buffer in (bz, rz):
                for i in range(ITERS):
                    clear("slab", buffer, i)
            for i in range(ITERS):
                clear("row", dext, i)
            for i in range(1, ITERS):
                clear("row", ext, i)
        for p in order:
            z_recv(it, 0, p)
            stage_ratio(it, p)
        for p in order[:-1]:
            z_recv(it, 1, p)
            stage_zy(it, p)
        if it < ITERS - 1:
            for p in range(chunks - 2):
                stage_x(it, p)
            for p in range(chunks - 3):
                stage_xy(it + 1, p)
            z_recv(it, 1, order[-1])
            stage_zy(it, order[-1])
            stage_x(it, chunks - 2)
            stage_xy(it + 1, chunks - 3)
            stage_x(it, chunks - 1)
            started = chunks - 2
        else:
            early = [p for p in range(chunks) if abs(p - order[-1]) > 1]
            for p in early:
                stage_x(it, p)
            z_recv(it, 1, order[-1])
            stage_zy(it, order[-1])
            for p in range(chunks):
                if p not in early:
                    stage_x(it, p)

    for axis, side, make in sends:
        sent(axis, side, make)


def solution(mesh):
    rows_n, slabs_n = mesh.shape["row"], mesh.shape["slab"]

    def on_device(observed, band_index, taps_x, taps_y, taps_z):
        depth, height, width = observed.shape
        bands, taps = taps_x.shape
        radius = taps // 2

        vmem = pl.BlockSpec(memory_space=pltpu.VMEM)
        hbm = pl.BlockSpec(memory_space=pltpu.HBM)
        chunks = height // CHUNK
        return pl.pallas_call(
            functools.partial(kernel, rows_n, slabs_n, taps),
            out_shape=jax.ShapeDtypeStruct(observed.shape, F32),
            in_specs=[hbm] * 5,
            out_specs=vmem,
            scratch_shapes=[
                pltpu.SMEM((depth,), jnp.int32),
                pltpu.SMEM((taps,), F32),
                pltpu.VMEM((bands, taps), F32),
                pltpu.VMEM((bands, taps), F32),
                pltpu.SemaphoreType.DMA((5,)),
            ] + [pltpu.VMEM((bands, LANES), F32)] * 4 + [
                pltpu.VMEM((ITERS, depth, height + 2 * CHUNK, width), F32),
                pltpu.VMEM((ITERS, depth, height + 2 * CHUNK, width), F32),
                pltpu.VMEM((ITERS, depth + 2 * radius, height, width), F32),
                pltpu.VMEM((ITERS, depth + 2 * radius, height, width), F32),
                pltpu.VMEM((depth, width, width), BF16),
                pltpu.VMEM((depth, width, width), BF16),
                pltpu.VMEM((depth, width, width), BF16),
                pltpu.VMEM((depth, width, width), BF16),
                pltpu.VMEM((depth, CHUNK, width), BF16),
                pltpu.VMEM((depth, chunks, CHUNK, width), BF16),
                pltpu.SemaphoreType.DMA((ITERS, 2, chunks, 2)),
                pltpu.SemaphoreType.DMA((ITERS, 2, chunks, 2)),
                pltpu.SemaphoreType.DMA((ITERS, 2, 2)),
                pltpu.SemaphoreType.DMA((ITERS, 2, 2)),
            ],
            compiler_params=pltpu.CompilerParams(
                collective_id=0, has_side_effects=True, vmem_limit_bytes=63 * 1024 * 1024 + 900 * 1024
            ),
        )(
            band_index, taps_z, taps_x, taps_y,
            observed,
        )

    in_specs = (P(("grp", "slab"), "row", None), P("slab"), P(), P(), P())
    return jax.shard_map(
        on_device, mesh=mesh, in_specs=in_specs, out_specs=P(("grp", "slab"), "row", None), check_vma=False
    )
```

```python
import functools

import jax
import jax.numpy as jnp
from jax import lax
from jax.experimental import pallas as pl
from jax.experimental.pallas import tpu as pltpu
from jax.sharding import PartitionSpec as P

ITERS = 2
CHUNK = 16
LANES = 128
F32 = jnp.float32
BF16 = jnp.bfloat16


def split(v):
    high = v.astype(BF16)
    return high, (v - high.astype(F32)).astype(BF16)


def chunk_order(count, it):
    first = [1, 0] if it == 0 else [0, 1]
    inner = list(range(2, count - 1))
    return first + ([count - 1] + inner if it == ITERS - 1 else inner + [count - 1])


def kernel(
    rows_n, slabs_n, taps,
    band_hbm, tz_hbm, tx_hbm, ty_hbm, obs_hbm,
    out_ref,
    band_ref, tz_ref, tx_ref, ty_ref, in_sem,
    txf_ref, txr_ref, tyf_ref, tyr_ref, ext, dext, bz, rz, wf_h, wf_l, wa_h, wa_l, af, aa,
    zs_sem, zr_sem, xs_sem, xr_sem,
):
    depth, height, width = obs_hbm.shape
    radius = taps // 2
    halo = CHUNK
    chunks = height // CHUNK
    row = lax.axis_index("row")
    slab = lax.axis_index("slab")
    parity = row % 2

    def chunk(p):
        return p + parity * (chunks - 1 - 2 * p)

    def begin(p, more=0, unit=CHUNK):
        return pl.multiple_of(chunk(p) * CHUNK + more, unit)

    fetches = [
        pltpu.make_async_copy(src, dst, in_sem.at[n])
        for n, (src, dst) in enumerate((
            (obs_hbm, ext.at[0, :, pl.ds(halo, height), :]),
            (ty_hbm, ty_ref), (tx_hbm, tx_ref), (band_hbm, band_ref), (tz_hbm, tz_ref),
        ))
    ]
    for fetch in fetches:
        fetch.start()

    sides = {
        ("row", 0): (row < rows_n - 1, row + 1),
        ("row", 1): (row > 0, row - 1),
        ("slab", 0): (slab < slabs_n - 1, slab + 1),
        ("slab", 1): (slab > 0, slab - 1),
    }

    barrier = pltpu.get_barrier_semaphore()
    for (axis, _), (there, index) in sides.items():
        @pl.when(there)
        def _(axis=axis, index=index):
            pl.semaphore_signal(barrier, inc=1, device_id={axis: index}, device_id_type=pl.DeviceIdType.MESH)

    def clear(axis, buffer, it):
        for side in range(2):
            @pl.when(jnp.logical_not(sides[(axis, side)][0]))
            def _():
                if axis == "row":
                    first = 0 if side == 1 else halo + height
                    buffer[it, :, first:first + halo, :] = jnp.zeros((depth, halo, width), F32)
                else:
                    first = 0 if side == 1 else radius + depth
                    buffer[it, first:first + radius] = jnp.zeros((radius, height, width), F32)

    pl.semaphore_wait(barrier, sum(there.astype(jnp.int32) for there, _ in sides.values()))

    def row_copy(src, dst, it, which, side):
        if side == 0:
            src_start, dst_start = src[1] + height - halo, 0
        else:
            src_start, dst_start = src[1], halo + height
        return pltpu.make_async_remote_copy(
            src_ref=src[0].at[:, pl.ds(src_start, halo), :],
            dst_ref=dst.at[it, :, pl.ds(dst_start, halo), :],
            send_sem=xs_sem.at[it, which, side],
            recv_sem=xr_sem.at[it, which, side],
            device_id={"row": sides[("row", side)][1]},
            device_id_type=pl.DeviceIdType.MESH,
        )

    def slab_copy(buf, it, which, c, side):
        if side == 0:
            src_start, dst_start = depth, 0
        else:
            src_start, dst_start = radius, radius + depth
        span = pl.ds(begin(c), CHUNK)
        return pltpu.make_async_remote_copy(
            src_ref=buf.at[it, pl.ds(src_start, radius), span, :],
            dst_ref=buf.at[it, pl.ds(dst_start, radius), span, :],
            send_sem=zs_sem.at[it, which, c, side],
            recv_sem=zr_sem.at[it, which, c, side],
            device_id={"slab": sides[("slab", side)][1]},
            device_id_type=pl.DeviceIdType.MESH,
        )

    def start(axis, side, make, also=True):
        @pl.when(sides[(axis, side)][0] & also)
        def _():
            make(side).start()

    def recv(axis, side, make, also=True):
        @pl.when(sides[(axis, 1 - side)][0] & also)
        def _():
            make(side).wait_recv()

    def sent(axis, side, make):
        @pl.when(sides[(axis, side)][0])
        def _():
            make(side).wait_send()

    sends = []

    def x_make(it, which):
        buffer = ext if which == 0 else dext
        return functools.partial(row_copy, (buffer.at[it], halo), buffer, it, which)

    def z_make(it, which, c):
        return functools.partial(slab_copy, bz if which == 0 else rz, it, which, c)

    def x_start(it, which, p):
        near = p == 0
        for v in range(2):
            side = 1 - v if near else v
            start("row", side, x_make(it, which), parity == v)
        if near:
            sends.extend(("row", side, x_make(it, which)) for side in range(2))

    def x_recv(it, which, p):
        near = p == 0
        for v in range(2):
            recv("row", v if near else 1 - v, x_make(it, which), parity == v)

    def z_start(it, which, c):
        for side in range(2):
            start("slab", side, z_make(it, which, c))
            sends.append(("slab", side, z_make(it, which, c)))

    def z_recv(it, which, c):
        for side in range(2):
            recv("slab", side, z_make(it, which, c))

    fetches[0].wait()
    for p in (0, chunks - 1):
        x_start(0, 0, p)
    for fetch in fetches[1:]:
        fetch.wait()

    kk = 3 * halo
    mirror = (
        lax.broadcasted_iota(jnp.int32, (LANES, LANES), 0) + lax.broadcasted_iota(jnp.int32, (LANES, LANES), 1)
        == taps - 1
    ).astype(F32)
    for source, ahead, back in ((tx_ref, txf_ref, txr_ref), (ty_ref, tyf_ref, tyr_ref)):
        ahead[...] = jnp.zeros(ahead.shape, F32)
        ahead[:, 0:taps] = source[...]
        back[...] = jnp.dot(ahead[...], mirror, precision=lax.Precision.HIGHEST, preferred_element_type=F32)

    gap = lax.broadcasted_iota(jnp.int32, (LANES, LANES), 0) - lax.broadcasted_iota(jnp.int32, (LANES, LANES), 1)
    blocks = range(width // LANES)

    def column_band(line):
        ring = pltpu.roll(jnp.broadcast_to(line, (LANES, LANES)), LANES - radius, 1, stride=1, stride_axis=0)

        def block(offset):
            near = gap + offset * LANES
            return jnp.where((near <= radius) & (near >= -radius), ring, 0.0)
        made = {offset: block(offset) for offset in (-1, 0, 1)}
        return [[made.get(i - j) for j in blocks] for i in blocks]

    def store_band(w_h, w_l, z, band, scale):
        for i in blocks:
            for j in blocks:
                part = jnp.zeros((LANES, LANES), F32) if band[i][j] is None else band[i][j]
                if scale is not None:
                    part = part * scale[j]
                high, low = split(part)
                w_h[z, i * LANES:(i + 1) * LANES, j * LANES:(j + 1) * LANES] = high
                w_l[z, i * LANES:(i + 1) * LANES, j * LANES:(j + 1) * LANES] = low

    def store_rows(a):
        high = a.astype(BF16).astype(F32)
        low = a - high
        zero = jnp.zeros(a.shape, F32)
        first = jnp.concatenate([high, zero], axis=1)
        second = jnp.concatenate([low, zero], axis=1)
        return (first + pltpu.roll(second, kk, 1) + pltpu.roll(first, 2 * kk, 1)).astype(BF16)

    def row_band(line):
        return pltpu.roll(jnp.broadcast_to(line, (CHUNK, LANES)), halo - radius, 1, stride=1, stride_axis=0)

    def build_forward(z, carry):
        at = pl.ds(band_ref[z], 1)
        store_band(wf_h, wf_l, z, column_band(tyr_ref[at, :]), None)
        af[z] = store_rows(row_band(txf_ref[at, :]))
        return carry

    def build_adjoint(z, carry):
        at = pl.ds(band_ref[z], 1)
        band = column_band(tyf_ref[at, :])
        lane = lax.broadcasted_iota(jnp.int32, (1, LANES), 1)
        tzv = jnp.zeros((1, LANES), F32)
        for k in range(taps):
            tzv = jnp.where(lane == k, tz_ref[k], tzv)
        plane = slab * depth + z + radius - lane
        inside = (plane >= 0) & (plane < slabs_n * depth)
        cz = jnp.sum(jnp.where(inside, tzv, 0.0), axis=1, keepdims=True)
        scale = []
        for j in blocks:
            total = sum(jnp.sum(band[i][j], axis=0, keepdims=True) for i in blocks if band[i][j] is not None)
            scale.append(1.0 / (total * cz))
        store_band(wa_h, wa_l, z, band, scale)
        base = row_band(txr_ref[at, :])
        for c in range(chunks):
            at_row = row * height + (c - 1) * CHUNK + lax.broadcasted_iota(jnp.int32, (CHUNK, LANES), 1)
            inside = (at_row >= 0) & (at_row < rows_n * height)
            aa[z, c] = store_rows(base / jnp.sum(jnp.where(inside, base, 0.0), axis=1, keepdims=True))
        return carry

    def blur_rows(a, v):
        high, low = split(v)
        return jnp.dot(a[:, :3 * kk], jnp.concatenate([high, high, low], axis=0), preferred_element_type=F32)

    def blur_columns(v, w_h, w_l):
        high, low = split(v)
        n = v.shape[0]
        both = jnp.dot(jnp.concatenate([high, low], axis=0), w_h, preferred_element_type=F32)
        return both[:n] + both[n:] + jnp.dot(high, w_l, preferred_element_type=F32)

    def edge(it, which, p):
        if p in (0, chunks - 1):
            x_recv(it, which, p)

    def stage_xy(it, p):
        edge(it, 0, p)
        c = begin(p)

        def body(z, carry):
            v = blur_rows(af[z], ext[it, z, pl.ds(c, kk), :])
            bz[it, radius + z, pl.ds(c, CHUNK), :] = blur_columns(v, wf_h[z], wf_l[z])
            return carry
        lax.fori_loop(0, depth, body, 0, unroll=8)
        z_start(it, 0, p)

    def blur_depth(buf, it, tile, lanes, flip):
        total = None
        for k in range(taps):
            weight = tz_ref[taps - 1 - k] if flip else tz_ref[k]
            term = weight * buf[it, k:k + depth, tile, lanes]
            total = term if total is None else total + term
        return total

    def tiles(p):
        for r in range(0, CHUNK, 8):
            for l in range(0, width, LANES):
                yield pl.ds(begin(p, r, 8), 8), pl.ds(begin(p, halo + r, 8), 8), slice(l, l + LANES)

    def stage_ratio(it, p):
        for tile, inner, lanes in tiles(p):
            blurred = blur_depth(bz, it, tile, lanes, False)
            rz[it, radius:radius + depth, tile, lanes] = ext[0, :, inner, lanes] / blurred
        z_start(it, 1, p)

    def stage_zy(it, p):
        for tile, inner, lanes in tiles(p):
            dext[it, :, inner, lanes] = blur_depth(rz, it, tile, lanes, True)
        rows = pl.ds(begin(p, halo), CHUNK)

        def body(z, carry):
            dext[it, z, rows, :] = blur_columns(dext[it, z, rows, :], wa_h[z], wa_l[z])
            return carry
        lax.fori_loop(0, depth, body, 0, unroll=8)
        if p in (0, chunks - 1):
            x_start(it, 1, p)

    def stage_x(it, p):
        edge(it, 1, p)
        c = begin(p)
        inner = pl.ds(begin(p, halo), CHUNK)

        def body(z, carry):
            v = ext[it, z, inner, :] * blur_rows(aa[z, chunk(p)], dext[it, z, pl.ds(c, kk), :])
            if it == ITERS - 1:
                out_ref[z, pl.ds(c, CHUNK), :] = v
            else:
                ext[it + 1, z, inner, :] = v
            return carry
        lax.fori_loop(0, depth, body, 0, unroll=8)
        if it < ITERS - 1 and p in (0, chunks - 1):
            x_start(it + 1, 0, p)

    clear("row", ext, 0)
    lax.fori_loop(0, depth, build_forward, 0, unroll=2)
    started = 0
    for it in range(ITERS):
        order = chunk_order(chunks, it)
        for p in order[started:]:
            stage_xy(it, p)
        if it == 0:
            lax.fori_loop(0, depth, build_adjoint, 0)
            for buffer in (bz, rz):
                for i in range(ITERS):
                    clear("slab", buffer, i)
            for i in range(ITERS):
                clear("row", dext, i)
            for i in range(1, ITERS):
                clear("row", ext, i)
        for p in order:
            z_recv(it, 0, p)
            stage_ratio(it, p)
        for p in order[:-1]:
            z_recv(it, 1, p)
            stage_zy(it, p)
        if it < ITERS - 1:
            for p in range(chunks - 2):
                stage_x(it, p)
            for p in range(chunks - 3):
                stage_xy(it + 1, p)
            z_recv(it, 1, order[-1])
            stage_zy(it, order[-1])
            stage_x(it, chunks - 2)
            stage_xy(it + 1, chunks - 3)
            stage_x(it, chunks - 1)
            started = chunks - 2
        else:
            early = [p for p in range(chunks) if abs(p - order[-1]) > 1]
            for p in early:
                stage_x(it, p)
            z_recv(it, 1, order[-1])
            stage_zy(it, order[-1])
            for p in range(chunks):
                if p not in early:
                    stage_x(it, p)

    for axis, side, make in sends:
        sent(axis, side, make)


def solution(mesh):
    rows_n, slabs_n = mesh.shape["row"], mesh.shape["slab"]

    def on_device(observed, band_index, taps_x, taps_y, taps_z):
        depth, height, width = observed.shape
        bands, taps = taps_x.shape
        radius = taps // 2

        vmem = pl.BlockSpec(memory_space=pltpu.VMEM)
        hbm = pl.BlockSpec(memory_space=pltpu.HBM)
        chunks = height // CHUNK
        return pl.pallas_call(
            functools.partial(kernel, rows_n, slabs_n, taps),
            out_shape=jax.ShapeDtypeStruct(observed.shape, F32),
            in_specs=[hbm] * 5,
            out_specs=vmem,
            scratch_shapes=[
                pltpu.SMEM((depth,), jnp.int32),
                pltpu.SMEM((taps,), F32),
                pltpu.VMEM((bands, taps), F32),
                pltpu.VMEM((bands, taps), F32),
                pltpu.SemaphoreType.DMA((5,)),
            ] + [pltpu.VMEM((bands, LANES), F32)] * 4 + [
                pltpu.VMEM((ITERS, depth, height + 2 * CHUNK, width), F32),
                pltpu.VMEM((ITERS, depth, height + 2 * CHUNK, width), F32),
                pltpu.VMEM((ITERS, depth + 2 * radius, height, width), F32),
                pltpu.VMEM((ITERS, depth + 2 * radius, height, width), F32),
                pltpu.VMEM((depth, width, width), BF16),
                pltpu.VMEM((depth, width, width), BF16),
                pltpu.VMEM((depth, width, width), BF16),
                pltpu.VMEM((depth, width, width), BF16),
                pltpu.VMEM((depth, CHUNK, width), BF16),
                pltpu.VMEM((depth, chunks, CHUNK, width), BF16),
                pltpu.SemaphoreType.DMA((ITERS, 2, chunks, 2)),
                pltpu.SemaphoreType.DMA((ITERS, 2, chunks, 2)),
                pltpu.SemaphoreType.DMA((ITERS, 2, 2)),
                pltpu.SemaphoreType.DMA((ITERS, 2, 2)),
            ],
            compiler_params=pltpu.CompilerParams(
                collective_id=0, has_side_effects=True, vmem_limit_bytes=63 * 1024 * 1024 + 900 * 1024
            ),
        )(
            band_index, taps_z, taps_x, taps_y,
            observed,
        )

    in_specs = (P(("grp", "slab"), "row", None), P("slab"), P(), P(), P())
    return jax.shard_map(
        on_device, mesh=mesh, in_specs=in_specs, out_specs=P(("grp", "slab"), "row", None), check_vma=False
    )
```
